32 devices in a mesh: dp: 2 (over y), ctx: 2 (over x), exp: 8 (over z, core).
Axes of the slice: x: 2, y: 2, z: 4, core: 2. Of those that a mesh axis runs over, the one named last changes fastest.
Arguments:
- queries: bfloat16 [512, 4096], P(('dp', 'ctx'), 'exp'), parts along dimension 0, may hold values from -6 to 6
- key_vecs: bfloat16 [512, 4096], P(('dp', 'ctx'), 'exp'), parts along dimension 0, may hold values from -6 to 6
- values: bfloat16 [512, 4096], P(('dp', 'ctx'), 'exp'), parts along dimension 0, may hold values from -6 to 6
- residual: bfloat16 [512, 6144], P(('dp', 'ctx', 'exp')), parts along dimension 0, may hold values from -6 to 6
- out_weight: bfloat16 [4096, 6144], P('exp', 'ctx'), may hold values from -0.09375 to 0.09375
- router_weight: bfloat16 [6144, 4], replicated, may hold values from -0.078125 to 0.078125
- expert_ids: int32 [512, 2], P(('dp', 'ctx', 'exp')), parts along dimension 0, may hold values from 0 to 3, all different within a row; in each aligned block of 16 rows (0 to 15, 16 to 31, ...) at most 12 rows name the same one
- gate_weight: bfloat16 [8, 6144, 2304], P('exp', None, 'ctx'), may hold values from -0.078125 to 0.078125
- up_weight: bfloat16 [8, 6144, 2304], P('exp', None, 'ctx'), may hold values from -0.078125 to 0.078125
- down_weight: bfloat16 [8, 2304, 6144], P('exp', 'ctx'), may hold values from -0.09375 to 0.09375
Outputs:
- layer_out: bfloat16 [512, 6144], P(('dp', 'ctx', 'exp')), parts along dimension 0
The draws below stay inside these ranges and needn't reach their ends.
There are 2 independent parts, one for each index of `dp`. The reference program is written for one: setup_inputs(seed, part) draws one part's arguments, and reference() takes and returns one part's arrays. A program takes and returns all parts, laid end to end along the dimension named above; an argument that names none is the same for every part. Nothing has to cross between parts.
Inputs may be any that keep to these rules, and one draw needn't show every extreme that they name: `expert_ids`: the two experts of a row differ. In each aligned block of 16 rows (the rows of one device) no expert is named by more than 12 rows.
All inputs are finite; a program needn't handle non-finite values.
Results may differ from the reference program's by a relative error of at most 0.017.
Values may be sent and summed in bfloat16 or wider, within the bound.
A program may use at most 128 MiB of HBM per device.

```python
import math
import jax
import jax.numpy as jnp
import numpy as np
from jax import lax

D = 6144
HEAD = 128
HEADS = 32
HID = 4608
TOK_CTX = 128
ATT = 4096
SEQ = 256
EXPERTS = 4
TOK_MOE = 16
CAP = 12
N_CTX = 2
N_EXP = 8


def block_scale(stream_key, shape, split, low, top_value):
    level = 1.0
    for dim, shards_of in split:
        steps = jax.random.uniform(jax.random.fold_in(jax.random.fold_in(stream_key, 6), dim), (shards_of,), jnp.float32, low / len(split), top_value / len(split))
        level = level * jnp.repeat(jnp.exp(steps), shape[dim] // shards_of).reshape((-1,) + (1,) * (len(shape) - 1 - dim))
    return level


def assign_block(key, own, number, rows, amount, top, most, lean):
    sequence = jax.random.permutation(key, amount)
    crowded, ordinary = portions_of(amount, rows * top, most, lean, True), portions_of(amount, rows * top, most, lean, False)
    places = jnp.arange(amount)

    def named(tallies, rotation):
        used = int((tallies > 0).sum())
        fixed = max(1, used // 4)
        shifted = fixed + (places - fixed + rotation * (used - fixed)) % max(1, amount - fixed)
        return jnp.zeros((amount,), jnp.int32).at[sequence[jnp.where(places < fixed, places, shifted)]].set(jnp.asarray(tallies, jnp.int32))

    tallies = jnp.where(number % 4 == 0, named(crowded, number // 4), named(ordinary, number - number // 4 - 1))
    mixed = jax.random.permutation(jax.random.fold_in(own, 3), amount)
    source_of, taker = mixed[0:amount // 2 * 2:2], mixed[1:amount // 2 * 2:2]
    room = jnp.minimum(tallies[source_of] - 1, most - tallies[taker]) // 2
    room = jnp.where((source_of == sequence[0]) | (taker == sequence[0]) | (tallies[taker] == 0), 0, jnp.maximum(room, 0))
    shifted = jax.random.randint(jax.random.fold_in(own, 4), (amount // 2,), 0, 1 << 20) % (room + 1)
    tallies = tallies.at[source_of].add(-shifted).at[taker].add(shifted)
    items = jnp.searchsorted(jnp.cumsum(tallies), jnp.arange(rows * top), side="right").astype(jnp.int32)
    grid = items.reshape(top, rows).T
    grid = grid[jax.random.permutation(jax.random.fold_in(own, 1), rows)]
    rotation = jax.random.randint(jax.random.fold_in(own, 2), (rows, 1), 0, top)
    return jnp.take_along_axis(grid, (jnp.arange(top)[None, :] + rotation) % top, axis=1)


def portions_of(count, total, most, slope, full):
    weights = [(1 << 20) // math.isqrt(standing ** slope) + 1 for standing in range(1, count + 1)]
    largest = most if full else min(most, max(-(-total // count), total * weights[0] // sum(weights)))
    least = 1 if total - largest >= count - 1 else 0
    given, surplus = [largest] + [least] * (count - 1), total - largest - least * (count - 1)
    while surplus > 0:
        movable = [i for i in range(1, count) if given[i] < largest] or [i for i in range(1, count) if given[i] < most]
        whole, remaining = sum([weights[i] for i in movable]), surplus
        for i in movable:
            extra = min(most - given[i], max(1, remaining * weights[i] // whole), surplus)
            given[i] = given[i] + extra
            surplus = surplus - extra
    return np.array(given)


def scatter_about(own_key, shape, spread, limit, pieces=(), dtype=jnp.bfloat16):
    result = jax.random.normal(own_key, shape, jnp.float32) * spread
    if len(pieces) > 0:
        result = block_scale(own_key, shape, pieces, -0.22, 0.18) * result
    return jnp.clip(result, min=-limit, max=limit).astype(dtype)


def setup_inputs(seed: int = 0, part: int = 0) -> dict:
    key_of = jax.random.split(jax.random.key(seed), 11)
    part_keys = jax.random.split(jax.random.fold_in(key_of[10], part), 11)
    queries = scatter_about(part_keys[0], (SEQ, ATT), 1.0, 6.0, ((0, 2), (1, 8)))
    key_vecs = scatter_about(part_keys[1], (SEQ, ATT), 1.0, 6.0, ((0, 2), (1, 8)))
    values = scatter_about(part_keys[2], (SEQ, ATT), 1.0, 6.0, ((0, 2), (1, 8)))
    residual = scatter_about(part_keys[3], (SEQ, D), 1.0, 6.0, ((0, 16),))
    out_weight = scatter_about(key_of[4], (ATT, D), ATT ** -0.5, 0.09375, ((0, 8), (1, 2)))
    router_weight = scatter_about(key_of[5], (D, EXPERTS), D ** -0.5, 0.078125)
    expert_ids_keys = jax.random.split(jax.random.fold_in(part_keys[6], 1), SEQ // TOK_MOE)
    expert_ids_turns = jax.random.permutation(jax.random.fold_in(part_keys[6], 3), SEQ // TOK_MOE)
    expert_ids = jax.vmap(lambda own, number: assign_block(jax.random.fold_in(part_keys[6], 2), own, number, TOK_MOE, EXPERTS, 2, CAP, 2))(expert_ids_keys, expert_ids_turns).reshape((SEQ, 2))
    gate_weight = scatter_about(key_of[7], (2 * EXPERTS, D, HID // 2), D ** -0.5, 0.078125, ((0, 8), (2, 2)))
    up_weight = scatter_about(key_of[8], (2 * EXPERTS, D, HID // 2), D ** -0.5, 0.078125, ((0, 8), (2, 2)))
    down_weight = scatter_about(key_of[9], (2 * EXPERTS, HID // 2, D), HID ** -0.5, 0.09375, ((0, 8), (1, 2)))
    return {"queries": queries, "key_vecs": key_vecs, "values": values, "residual": residual, "out_weight": out_weight, "router_weight": router_weight, "expert_ids": expert_ids, "gate_weight": gate_weight, "up_weight": up_weight, "down_weight": down_weight}


EPSILON = 1e-06

def reference(queries, key_vecs, values, residual, out_weight, router_weight, expert_ids, gate_weight, up_weight, down_weight):
    q_blocks = queries.astype(jnp.float32).reshape(N_CTX, TOK_CTX, HEADS, HEAD)
    k_blocks = key_vecs.astype(jnp.float32).reshape(N_CTX, TOK_CTX, HEADS, HEAD)
    v_blocks = values.astype(jnp.float32).reshape(N_CTX, TOK_CTX, HEADS, HEAD)
    scores = jnp.einsum('cthd,cshd->chts', q_blocks, k_blocks)
    causal = jnp.arange(TOK_CTX)[:, None] >= jnp.arange(TOK_CTX)[None, :]
    masked = jnp.where(causal[None, None], scores, jnp.float32(0.0))
    masked = lax.optimization_barrier(masked.astype(jnp.bfloat16)).astype(jnp.float32)
    within = jnp.einsum('chts,cshd->cthd', masked, v_blocks)
    own_state = jnp.einsum('cshd,cshe->chde', k_blocks, v_blocks)
    running = jnp.cumsum(own_state, axis=0)
    earlier = jnp.concatenate([jnp.zeros_like(own_state[:1]), running[:-1]], axis=0)
    earlier = lax.optimization_barrier(earlier.astype(jnp.bfloat16)).astype(jnp.float32)
    carried = jnp.einsum('cthd,chde->cthe', q_blocks, earlier)
    attended = within + carried
    normed = attended * lax.rsqrt(lax.optimization_barrier(jnp.mean(attended * attended, axis=-1, keepdims=True)) + EPSILON)
    heads_out = normed.astype(jnp.bfloat16).reshape(SEQ, ATT)
    group_width = ATT // N_EXP
    mixed = jnp.zeros((SEQ, D), jnp.float32)
    for group in range(N_EXP):
        lower = group * group_width
        term = jnp.dot(heads_out[:, lower:lower + group_width], out_weight[lower:lower + group_width], preferred_element_type=jnp.float32)
        mixed = mixed + lax.optimization_barrier(term.astype(jnp.bfloat16)).astype(jnp.float32)
    hidden_in = (residual.astype(jnp.float32) + mixed).astype(jnp.bfloat16)
    logits = jnp.dot(hidden_in, router_weight, preferred_element_type=jnp.float32)
    picked = jnp.take_along_axis(logits, expert_ids, axis=1)
    leading = jax.nn.sigmoid(picked[:, 0] - picked[:, 1])
    slice_width = HID // 2 // N_CTX
    expert_out = jnp.zeros((SEQ, D), jnp.float32)
    for expert in range(EXPERTS):
        summed = jnp.zeros((SEQ, D), jnp.float32)
        for half in range(2):
            index = 2 * expert + half
            gate_part = jnp.dot(hidden_in, gate_weight[index], preferred_element_type=jnp.float32)
            up_part = jnp.dot(hidden_in, up_weight[index], preferred_element_type=jnp.float32)
            hidden = (jax.nn.silu(gate_part) * up_part).astype(jnp.bfloat16)
            for block in range(N_CTX):
                lower = block * slice_width
                piece = jnp.dot(hidden[:, lower:lower + slice_width], down_weight[index, lower:lower + slice_width], preferred_element_type=jnp.float32)
                summed = summed + lax.optimization_barrier(piece.astype(jnp.bfloat16)).astype(jnp.float32)
        share = leading * (expert_ids[:, 0] == expert).astype(jnp.float32) + (1.0 - leading) * (expert_ids[:, 1] == expert).astype(jnp.float32)
        expert_out = expert_out + share[:, None] * summed
    return (hidden_in.astype(jnp.float32) + expert_out).astype(jnp.bfloat16)
```

```python
import jax
import jax.numpy as jnp
from jax import lax
from jax.experimental import pallas as pl
from jax.experimental.pallas import tpu as pltpu
from jax.sharding import PartitionSpec as P

HEAD = 128


EPSILON = 1e-06


def carried_in(value, axis, combine, identity):
    peers, position = (lax.axis_size(axis), lax.axis_index(axis))
    everything = lax.all_gather(value.astype(jnp.bfloat16), axis)
    start = jnp.broadcast_to(jnp.asarray(identity, value.dtype), value.shape)

    def lap(k, before):
        reached = k < position
        new = combine(before, everything[k].astype(value.dtype))
        return jnp.where(reached, new, before)

    return lax.fori_loop(0, peers, lap, start)


def expert_rows(tokens, gate_half, up_half, down_half):
    gate_part = jnp.dot(tokens, gate_half, preferred_element_type=jnp.float32)
    up_part = jnp.dot(tokens, up_half, preferred_element_type=jnp.float32)
    hidden = (jax.nn.silu(gate_part) * up_part).astype(jnp.bfloat16)
    return jnp.dot(hidden, down_half, preferred_element_type=jnp.float32)


def add_states(first, second):
    return first + second


def per_device(
    queries,
    key_vecs,
    values,
    residual,
    out_weight,
    router_weight,
    expert_ids,
    gate_weight,
    up_weight,
    down_weight,
):
    ctx_count = lax.axis_size("ctx")
    exp_count = lax.axis_size("exp")
    span_len, local_width = queries.shape
    head_local = local_width // HEAD
    q_heads = queries.reshape(span_len, head_local, HEAD)
    k_heads = key_vecs.reshape(span_len, head_local, HEAD)
    v_heads = values.reshape(span_len, head_local, HEAD)
    scores = jnp.einsum("thd,shd->hts", q_heads, k_heads, preferred_element_type=jnp.float32)
    causal = jnp.arange(span_len)[:, None] >= jnp.arange(span_len)[None, :]
    masked = jnp.where(causal[None], scores, jnp.float32(0.0)).astype(jnp.bfloat16)
    within = jnp.einsum("hts,shd->thd", masked, v_heads, preferred_element_type=jnp.float32)
    own_state = jnp.einsum("shd,she->hde", k_heads, v_heads, preferred_element_type=jnp.float32)
    earlier = carried_in(own_state, "ctx", add_states, jnp.zeros_like(own_state))
    carried = jnp.einsum(
        "thd,hde->the", q_heads, earlier.astype(jnp.bfloat16), preferred_element_type=jnp.float32
    )
    attended = within + carried
    normed = attended * lax.rsqrt(jnp.mean(attended * attended, axis=-1, keepdims=True) + EPSILON)
    heads_out = normed.astype(jnp.bfloat16).reshape(span_len, local_width)
    projected = jnp.dot(
        heads_out,
        lax.all_gather(out_weight, "ctx", axis=1, tiled=True),
        preferred_element_type=jnp.float32,
    )
    mixed = lax.psum_scatter(
        projected.astype(jnp.bfloat16), "exp", scatter_dimension=0, tiled=True
    ).astype(jnp.float32)
    hidden_in = (residual.astype(jnp.float32) + mixed).astype(jnp.bfloat16)
    token_count, model_width = hidden_in.shape
    expert_count = router_weight.shape[1]
    capacity = min(token_count, 3 * token_count // expert_count)
    logits = jnp.dot(hidden_in, router_weight, preferred_element_type=jnp.float32)
    chosen = (expert_ids[:, :, None] == jnp.arange(expert_count)[None, None, :]).astype(jnp.float32)
    picked = jnp.sum(chosen * logits[:, None, :], axis=-1)
    leading = jax.nn.sigmoid(picked[:, 0] - picked[:, 1])
    mixing = jnp.stack([leading, 1.0 - leading], axis=1)
    entries = chosen.reshape(2 * token_count, expert_count)
    position = jnp.arange(2 * token_count)
    earlier_mask = (position[:, None] > position[None, :]).astype(jnp.float32)
    ranks = jnp.dot(earlier_mask, entries, precision=lax.Precision.HIGHEST)
    slot_of = jnp.sum(ranks * entries, axis=-1).reshape(token_count, 2)
    slot_hot = (
        slot_of[:, :, None] == jnp.arange(capacity).astype(jnp.float32)[None, None, :]
    ).astype(jnp.float32)
    placed = chosen[:, :, :, None] * slot_hot[:, :, None, :]
    dispatch = jnp.sum(placed, axis=1).astype(jnp.bfloat16)
    combine = jnp.sum(placed * mixing[:, :, None, None], axis=1)
    packed = jnp.einsum(
        "tes,td->esd", dispatch, hidden_in, preferred_element_type=jnp.float32
    ).astype(jnp.bfloat16)
    outgoing = jnp.repeat(packed, 2, axis=0)
    gate_half = gate_weight[0]
    up_half = up_weight[0]
    down_half = down_weight[0]
    fanned = jnp.broadcast_to(outgoing[None], (ctx_count,) + outgoing.shape).reshape(
        ctx_count * exp_count, capacity, model_width
    )
    arrived = lax.all_to_all(fanned, ("ctx", "exp"), split_axis=0, concat_axis=0, tiled=True)
    flattened = arrived.reshape(-1, model_width)
    partial_value = expert_rows(flattened, gate_half, up_half, down_half).reshape(arrived.shape)
    reduced = lax.psum_scatter(
        partial_value.reshape(ctx_count * exp_count * capacity, model_width).astype(jnp.bfloat16),
        "ctx",
        scatter_dimension=0,
        tiled=True,
    ).astype(jnp.float32)
    returned = lax.all_to_all(
        reduced.reshape(exp_count, capacity, model_width).astype(jnp.bfloat16),
        "exp",
        split_axis=0,
        concat_axis=0,
        tiled=True,
    ).astype(jnp.float32)
    summed = jnp.sum(returned.reshape(expert_count, 2, capacity, model_width), axis=1)
    expert_out = jnp.einsum(
        "tes,esd->td",
        combine,
        summed,
        precision=lax.Precision.HIGHEST,
        preferred_element_type=jnp.float32,
    )
    return (hidden_in.astype(jnp.float32) + expert_out).astype(jnp.bfloat16)


BF, F32 = jnp.bfloat16, jnp.float32
ROWS = 16


def layer_kernel(
    q_ref, k_ref, v_ref, res_ref, wo_hbm, router_ref, ids_ref, gate_hbm, up_hbm, down_hbm,
    out_ref,
    wy, gate, up, down, state, state_in, within, heads, res_in, term, pair_in, pair, ring_in,
    every, gate_sum, up_sum, hidden, core_in, side_out, side_in, ready, back,
    w_sem, att_s, att_r, pair_s, pair_r, ring_s, ring_r,
    gz_s, gz_r, gx_s, gx_r, gc_s, gc_r, yc_s, yc_r, yx_s, yx_r, yz_s, yz_r,
):
    h, e = lax.axis_index("ctx"), lax.axis_index("exp")
    z, c = e // 2, lax.rem(e, 2)
    half = res_ref.shape[1] // 2
    width = q_ref.shape[1]
    span = q_ref.shape[0]
    hid = gate.shape[1]
    chips = 4
    order = (2, 1, 3, 0)
    side = {"ctx": 1 - h, "exp": e}
    core = {"ctx": h, "exp": 2 * z + 1 - c}

    def at_z(dz):
        return lax.rem(z + dz, chips)

    def from_z(dz):
        return lax.rem(z + chips - dz, chips)

    def to(dz, other):
        return {"ctx": h, "exp": 2 * at_z(dz) + (1 - c if other else c)}

    started = []

    def link(src, dst, s, r, dev):
        return pltpu.make_async_remote_copy(
            src_ref=src, dst_ref=dst, send_sem=s, recv_sem=r, device_id=dev,
            device_id_type=pl.DeviceIdType.MESH,
        )

    def send(*args):
        copy = link(*args)
        copy.start()
        started.append(copy)
        return copy

    load_wo = pltpu.make_async_copy(wo_hbm, wy, w_sem.at[0])
    load_wo.start()
    loads = [
        pltpu.make_async_copy(gate_hbm.at[0], gate, w_sem.at[1]),
        pltpu.make_async_copy(up_hbm.at[0], up, w_sem.at[2]),
        pltpu.make_async_copy(down_hbm.at[0], down, w_sem.at[3]),
    ]

    barrier = pltpu.get_barrier_semaphore()
    pl.semaphore_signal(barrier, inc=1, device_id=side, device_id_type=pl.DeviceIdType.MESH)
    for dz in range(chips):
        for other in (False, True):
            if dz or other:
                pl.semaphore_signal(
                    barrier, inc=1, device_id=to(dz, other), device_id_type=pl.DeviceIdType.MESH
                )
    pl.semaphore_wait(barrier, 2 * chips)

    count = width // HEAD
    for i in range(count):
        cols = slice(i * HEAD, (i + 1) * HEAD)
        own = lax.dot_general(
            k_ref[:, cols], v_ref[:, cols], (((0,), (0,)), ((), ())), preferred_element_type=F32
        )
        state[cols, :] = own.astype(BF)
    state_copy = send(state, state_in, att_s.at[0], att_r.at[0], side)
    peer_cols = pl.ds(pl.multiple_of((1 - h) * half, half), half)
    my_cols = pl.ds(pl.multiple_of(h * half, half), half)
    res_copy = send(res_ref.at[:, peer_cols], res_in, att_s.at[1], att_r.at[1], side)
    keep = lax.broadcasted_iota(jnp.int32, (span, span), 0) >= lax.broadcasted_iota(
        jnp.int32, (span, span), 1
    )
    for i in range(count):
        cols = slice(i * HEAD, (i + 1) * HEAD)
        scores = lax.dot_general(
            q_ref[:, cols], k_ref[:, cols], (((1,), (1,)), ((), ())), preferred_element_type=F32
        )
        masked = jnp.where(keep, scores, 0.0).astype(BF)
        within[:, cols] = jnp.dot(masked, v_ref[:, cols], preferred_element_type=F32)
    state_copy.wait_recv()
    has_past = (h > 0).astype(F32)
    for i in range(count):
        cols = slice(i * HEAD, (i + 1) * HEAD)
        carried = jnp.dot(q_ref[:, cols], state_in[cols, :], preferred_element_type=F32)
        attended = within[:, cols] + carried * has_past
        normed = attended * lax.rsqrt(
            jnp.mean(attended * attended, axis=-1, keepdims=True) + EPSILON
        )
        heads[h, :, cols] = normed.astype(BF)
    heads_copy = send(heads.at[h], heads.at[h], att_s.at[2], att_r.at[2], side)
    for load in loads:
        load.start()
    load_wo.wait()

    tile = 256

    def project(b):
        @pl.loop(0, half // tile)
        def _(n):
            cols = pl.ds(pl.multiple_of(n * tile, tile), tile)
            part = jnp.dot(heads[b], wy[:, cols], preferred_element_type=F32).astype(BF)
            term[b, :, :, cols] = part.reshape(span // ROWS, ROWS, tile)

    project(h)
    link(heads.at[1 - h], heads.at[1 - h], att_s.at[2], att_r.at[2], side).wait_recv()
    project(1 - h)

    for dz in order:
        send(
            term.at[:, 2 * at_z(dz) + 1 - c], pair_in.at[dz], pair_s.at[dz], pair_r.at[dz], core
        )
    for dz in order:
        link(
            term.at[:, 2 * at_z(dz) + 1 - c], pair_in.at[dz], pair_s.at[dz], pair_r.at[dz], core
        ).wait_recv()
        if dz:
            both = term[:, 2 * at_z(dz) + c].astype(F32) + pair_in[dz].astype(F32)
            pair[dz - 1] = both.astype(BF)
            send(
                pair.at[dz - 1], ring_in.at[dz - 1], ring_s.at[dz - 1], ring_r.at[dz - 1],
                to(dz, False),
            )
    res_copy.wait_recv()
    for dz in (1, 2, 3):
        link(
            pair.at[dz - 1], ring_in.at[dz - 1], ring_s.at[dz - 1], ring_r.at[dz - 1],
            to(dz, False),
        ).wait_recv()

    def mixed(b):
        total = term[b, e].astype(F32) + pair_in[0, b].astype(F32)
        for dz in (1, 2, 3):
            total = total + ring_in[dz - 1, b].astype(F32)
        return total

    every[h, h, e] = (res_ref[:, my_cols].astype(F32) + mixed(h)).astype(BF)
    every[h, 1 - h, e] = (res_in[...].astype(F32) + mixed(1 - h)).astype(BF)

    def piece(side_half, owner):
        return every.at[side_half, :, owner]

    mine = piece(h, e)
    for dz in (2, 1, 3):
        send(mine, mine, gz_s.at[dz - 1], gz_r.at[dz - 1], to(dz, False))
    send(mine, mine, gx_s.at[0], gx_r.at[0], side)
    send(mine, mine, gc_s.at[0], gc_r.at[0], core)

    for dz in (1, 3, 2):
        owner = 2 * from_z(dz) + c
        got = piece(h, owner)
        link(got, got, gz_s.at[dz - 1], gz_r.at[dz - 1], to(dz, False)).wait_recv()
        send(got, got, gx_s.at[dz], gx_r.at[dz], side)
        send(got, got, gc_s.at[dz], gc_r.at[dz], core)

    def pass_on(dz):
        got = piece(1 - h, 2 * from_z(dz) + c)
        link(got, got, gx_s.at[dz], gx_r.at[dz], side).wait_recv()
        send(got, got, gc_s.at[4 + dz], gc_r.at[4 + dz], core)

    def from_core(side_half, slot, dz):
        got = piece(side_half, 2 * from_z(dz) + 1 - c)
        link(got, got, gc_s.at[slot], gc_r.at[slot], core).wait_recv()

    def tiles(body):
        whole = hid // tile

        @pl.loop(0, whole)
        def _(n):
            body(pl.ds(pl.multiple_of(n * tile, tile), tile))

        if hid % tile:
            body(pl.ds(whole * tile, hid % tile))

    def product(side_half, weight, cols):
        rows = pl.ds(pl.multiple_of(side_half * half, half), half)
        return jnp.dot(
            every[side_half].reshape(2 * span, half), weight[rows, cols],
            preferred_element_type=F32,
        )

    for dz in range(chips):
        from_core(h, dz, dz)
    pass_on(0)
    pass_on(1)
    loads[0].wait()

    def first_gate(cols):
        gate_sum[:, cols] = product(h, gate, cols)

    def first_up(cols):
        up_sum[:, cols] = product(h, up, cols)

    tiles(first_gate)
    pass_on(3)
    loads[1].wait()
    tiles(first_up)
    pass_on(2)
    for dz in range(chips):
        from_core(1 - h, 4 + dz, dz)

    def second(cols):
        g = gate_sum[:, cols] + product(1 - h, gate, cols)
        u = up_sum[:, cols] + product(1 - h, up, cols)
        hidden[:, cols] = (g / (1.0 + jnp.exp(-g)) * u).astype(BF)

    tiles(second)
    loads[2].wait()

    def lower(side_half):
        @pl.loop(0, half // tile)
        def _(n):
            cols = pl.ds(pl.multiple_of(side_half * half + n * tile, tile), tile)
            part = jnp.dot(hidden[...], down[:, cols], preferred_element_type=F32)
            rows = pl.ds(pl.multiple_of(side_half * 2 * span, 2 * span), 2 * span)
            wy[rows, pl.ds(pl.multiple_of(n * tile, tile), tile)] = part.astype(BF)

    def rows_of(side_half, b, dz):
        first = side_half * 2 * span + b * span + 2 * ROWS * at_z(dz)
        return pl.ds(pl.multiple_of(first, 2 * ROWS), 2 * ROWS)

    def core_link(dz, b):
        return (
            wy.at[rows_of(1 - c, b, dz)], core_in.at[dz, b], yc_s.at[dz, b], yc_r.at[dz, b], core
        )

    def away(dz):
        return core_link(dz, 1 - h)

    lower(1 - c)
    for dz in order:
        for b in range(2):
            send(*core_link(dz, b))
    lower(c)
    for dz in order:
        for b in range(2):
            link(*core_link(dz, b)).wait_recv()
        side_out[dz] = (
            wy[rows_of(c, 1 - h, dz)].astype(F32) + core_in[dz, 1 - h].astype(F32)
        ).astype(BF)
        send(side_out.at[dz], side_in.at[dz], yx_s.at[dz], yx_r.at[dz], side)

    def out_link(dz, other):
        if dz:
            part = 1 - c if other else c
            src = ready.at[dz, pl.ds(pl.multiple_of(part * ROWS, ROWS), ROWS)]
        else:
            src = ready.at[dz, pl.ds(pl.multiple_of((1 - c) * ROWS, ROWS), ROWS)]
        o = int(other)
        return (src, back.at[dz, o], yz_s.at[dz, o], yz_r.at[dz, o], to(dz, other))

    for dz in order:
        link(side_out.at[dz], side_in.at[dz], yx_s.at[dz], yx_r.at[dz], side).wait_recv()
        ready[dz] = (
            wy[rows_of(c, h, dz)].astype(F32)
            + core_in[dz, h].astype(F32)
            + side_in[dz].astype(F32)
        ).astype(BF)
        for other in (False, True):
            if dz or other:
                send(*out_link(dz, other))

    logits = jnp.zeros((ROWS, router_ref.shape[0]), F32)
    for s in range(2):
        logits = logits + lax.dot_general(
            every[s, h, e], router_ref[:, s * half:(s + 1) * half],
            (((1,), (1,)), ((), ())), preferred_element_type=F32,
        )
    lanes = lax.broadcasted_iota(jnp.int32, logits.shape, 1)
    one = (ids_ref[:, 0:1] == lanes).astype(F32)
    two = (ids_ref[:, 1:2] == lanes).astype(F32)
    gap = jnp.sum((one - two) * logits, axis=1, keepdims=True)
    leading = 1.0 / (1.0 + jnp.exp(-gap))
    share = leading * one + (1.0 - leading) * two

    def weight_of(dz):
        return jnp.sum(jnp.where(lanes == from_z(dz), share, 0.0), axis=1, keepdims=True)

    weights = [weight_of(dz) for dz in range(chips)]
    for other in (False, True):
        for dz in order:
            if dz or other:
                link(*out_link(dz, other)).wait_recv()
        part = 1 - c if other else c
        total = every[part, h, e].astype(F32)
        for dz in range(chips):
            if dz or other:
                value = back[dz, int(other)]
            else:
                value = ready[0, pl.ds(pl.multiple_of(c * ROWS, ROWS), ROWS)]
            total = total + weights[dz] * value.astype(F32)
        out_ref[:, pl.ds(pl.multiple_of(part * half, half), half)] = total.astype(BF)
    for copy in started:
        copy.wait_send()


def per_device_fused(
    queries, key_vecs, values, residual, out_weight, router_weight, expert_ids,
    gate_weight, up_weight, down_weight,
):
    span, width = queries.shape
    half = out_weight.shape[1]
    model = residual.shape[1]
    hid = gate_weight.shape[2]
    blocks = span // ROWS
    vmem, sem = pltpu.VMEM, pltpu.SemaphoreType.DMA
    in_vmem = pl.BlockSpec(memory_space=pltpu.VMEM)
    in_hbm = pl.BlockSpec(memory_space=pl.ANY)
    return pl.pallas_call(
        layer_kernel,
        out_shape=jax.ShapeDtypeStruct(residual.shape, BF),
        in_specs=[in_vmem] * 4 + [in_hbm] + [in_vmem] * 2 + [in_hbm] * 3,
        out_specs=in_vmem,
        scratch_shapes=[
            vmem((width, half), BF),
            vmem((model, hid), BF),
            vmem((model, hid), BF),
            vmem((hid, model), BF),
            vmem((width, HEAD), BF),
            vmem((width, HEAD), BF),
            vmem((span, width), F32),
            vmem((2, span, width), BF),
            vmem((ROWS, half), BF),
            vmem((2, blocks, ROWS, half), BF),
            vmem((4, 2, ROWS, half), BF),
            vmem((3, 2, ROWS, half), BF),
            vmem((3, 2, ROWS, half), BF),
            vmem((2, 2, blocks, ROWS, half), BF),
            vmem((2 * span, hid), F32),
            vmem((2 * span, hid), F32),
            vmem((2 * span, hid), BF),
            vmem((4, 2, 2 * ROWS, half), BF),
            vmem((4, 2 * ROWS, half), BF),
            vmem((4, 2 * ROWS, half), BF),
            vmem((4, 2 * ROWS, half), BF),
            vmem((4, 2, ROWS, half), BF),
            sem((4,)), sem((3,)), sem((3,)), sem((4,)), sem((4,)), sem((3,)), sem((3,)),
            sem((3,)), sem((3,)), sem((4,)), sem((4,)), sem((8,)), sem((8,)),
            sem((4, 2)), sem((4, 2)), sem((4,)), sem((4,)), sem((4, 2)), sem((4, 2)),
        ],
        compiler_params=pltpu.CompilerParams(
            collective_id=0, has_side_effects=True, vmem_limit_bytes=VMEM_BYTES
        ),
    )(
        queries, key_vecs, values, residual, out_weight, router_weight.T, expert_ids,
        gate_weight, up_weight, down_weight,
    )


VMEM_BYTES = 66 * 1000 * 1000


def solution(mesh):
    fused = mesh.shape["ctx"] == 2 and mesh.shape["exp"] == 8
    body = per_device_fused if fused else per_device
    in_specs = (
        P(("dp", "ctx"), "exp"),
        P(("dp", "ctx"), "exp"),
        P(("dp", "ctx"), "exp"),
        P(("dp", "ctx", "exp"), None),
        P("exp", "ctx"),
        P(),
        P(("dp", "ctx", "exp"), None),
        P("exp", None, "ctx"),
        P("exp", None, "ctx"),
        P("exp", "ctx", None),
    )
    out_specs = P(("dp", "ctx", "exp"), None)
    return jax.shard_map(
        body, mesh=mesh, in_specs=in_specs, out_specs=out_specs, check_vma=False
    )
```

```python
import jax
import jax.numpy as jnp
from jax import lax
from jax.experimental import pallas as pl
from jax.experimental.pallas import tpu as pltpu
from jax.sharding import PartitionSpec as P

HEAD = 128


EPSILON = 1e-06


def carried_in(value, axis, combine, identity):
    peers, position = (lax.axis_size(axis), lax.axis_index(axis))
    everything = lax.all_gather(value.astype(jnp.bfloat16), axis)
    start = jnp.broadcast_to(jnp.asarray(identity, value.dtype), value.shape)

    def lap(k, before):
        reached = k < position
        new = combine(before, everything[k].astype(value.dtype))
        return jnp.where(reached, new, before)

    return lax.fori_loop(0, peers, lap, start)


def expert_rows(tokens, gate_half, up_half, down_half):
    gate_part = jnp.dot(tokens, gate_half, preferred_element_type=jnp.float32)
    up_part = jnp.dot(tokens, up_half, preferred_element_type=jnp.float32)
    hidden = (jax.nn.silu(gate_part) * up_part).astype(jnp.bfloat16)
    return jnp.dot(hidden, down_half, preferred_element_type=jnp.float32)


def add_states(first, second):
    return first + second


def per_device(
    queries,
    key_vecs,
    values,
    residual,
    out_weight,
    router_weight,
    expert_ids,
    gate_weight,
    up_weight,
    down_weight,
):
    ctx_count = lax.axis_size("ctx")
    exp_count = lax.axis_size("exp")
    span_len, local_width = queries.shape
    head_local = local_width // HEAD
    q_heads = queries.reshape(span_len, head_local, HEAD)
    k_heads = key_vecs.reshape(span_len, head_local, HEAD)
    v_heads = values.reshape(span_len, head_local, HEAD)
    scores = jnp.einsum("thd,shd->hts", q_heads, k_heads, preferred_element_type=jnp.float32)
    causal = jnp.arange(span_len)[:, None] >= jnp.arange(span_len)[None, :]
    masked = jnp.where(causal[None], scores, jnp.float32(0.0)).astype(jnp.bfloat16)
    within = jnp.einsum("hts,shd->thd", masked, v_heads, preferred_element_type=jnp.float32)
    own_state = jnp.einsum("shd,she->hde", k_heads, v_heads, preferred_element_type=jnp.float32)
    earlier = carried_in(own_state, "ctx", add_states, jnp.zeros_like(own_state))
    carried = jnp.einsum(
        "thd,hde->the", q_heads, earlier.astype(jnp.bfloat16), preferred_element_type=jnp.float32
    )
    attended = within + carried
    normed = attended * lax.rsqrt(jnp.mean(attended * attended, axis=-1, keepdims=True) + EPSILON)
    heads_out = normed.astype(jnp.bfloat16).reshape(span_len, local_width)
    projected = jnp.dot(
        heads_out,
        lax.all_gather(out_weight, "ctx", axis=1, tiled=True),
        preferred_element_type=jnp.float32,
    )
    mixed = lax.psum_scatter(
        projected.astype(jnp.bfloat16), "exp", scatter_dimension=0, tiled=True
    ).astype(jnp.float32)
    hidden_in = (residual.astype(jnp.float32) + mixed).astype(jnp.bfloat16)
    token_count, model_width = hidden_in.shape
    expert_count = router_weight.shape[1]
    capacity = min(token_count, 3 * token_count // expert_count)
    logits = jnp.dot(hidden_in, router_weight, preferred_element_type=jnp.float32)
    chosen = (expert_ids[:, :, None] == jnp.arange(expert_count)[None, None, :]).astype(jnp.float32)
    picked = jnp.sum(chosen * logits[:, None, :], axis=-1)
    leading = jax.nn.sigmoid(picked[:, 0] - picked[:, 1])
    mixing = jnp.stack([leading, 1.0 - leading], axis=1)
    entries = chosen.reshape(2 * token_count, expert_count)
    position = jnp.arange(2 * token_count)
    earlier_mask = (position[:, None] > position[None, :]).astype(jnp.float32)
    ranks = jnp.dot(earlier_mask, entries, precision=lax.Precision.HIGHEST)
    slot_of = jnp.sum(ranks * entries, axis=-1).reshape(token_count, 2)
    slot_hot = (
        slot_of[:, :, None] == jnp.arange(capacity).astype(jnp.float32)[None, None, :]
    ).astype(jnp.float32)
    placed = chosen[:, :, :, None] * slot_hot[:, :, None, :]
    dispatch = jnp.sum(placed, axis=1).astype(jnp.bfloat16)
    combine = jnp.sum(placed * mixing[:, :, None, None], axis=1)
    packed = jnp.einsum(
        "tes,td->esd", dispatch, hidden_in, preferred_element_type=jnp.float32
    ).astype(jnp.bfloat16)
    outgoing = jnp.repeat(packed, 2, axis=0)
    gate_half = gate_weight[0]
    up_half = up_weight[0]
    down_half = down_weight[0]
    fanned = jnp.broadcast_to(outgoing[None], (ctx_count,) + outgoing.shape).reshape(
        ctx_count * exp_count, capacity, model_width
    )
    arrived = lax.all_to_all(fanned, ("ctx", "exp"), split_axis=0, concat_axis=0, tiled=True)
    flattened = arrived.reshape(-1, model_width)
    partial_value = expert_rows(flattened, gate_half, up_half, down_half).reshape(arrived.shape)
    reduced = lax.psum_scatter(
        partial_value.reshape(ctx_count * exp_count * capacity, model_width).astype(jnp.bfloat16),
        "ctx",
        scatter_dimension=0,
        tiled=True,
    ).astype(jnp.float32)
    returned = lax.all_to_all(
        reduced.reshape(exp_count, capacity, model_width).astype(jnp.bfloat16),
        "exp",
        split_axis=0,
        concat_axis=0,
        tiled=True,
    ).astype(jnp.float32)
    summed = jnp.sum(returned.reshape(expert_count, 2, capacity, model_width), axis=1)
    expert_out = jnp.einsum(
        "tes,esd->td",
        combine,
        summed,
        precision=lax.Precision.HIGHEST,
        preferred_element_type=jnp.float32,
    )
    return (hidden_in.astype(jnp.float32) + expert_out).astype(jnp.bfloat16)


BF, F32 = jnp.bfloat16, jnp.float32
ROWS = 16


def layer_kernel(
    q_ref, k_ref, v_ref, res_ref, wo_hbm, router_ref, ids_ref, gate_hbm, up_hbm, down_hbm,
    out_ref,
    wy, gate, up, down, state, state_in, within, heads, res_in, term, pair_in, pair, ring_in,
    every, gate_sum, up_sum, hidden, core_in, side_out, side_in, ready, back,
    w_sem, state_s, state_r, heads_s, heads_r, att_s, att_r, pair_s, pair_r, ring_s, ring_r,
    gz_s, gz_r, gx_s, gx_r, gc_s, gc_r, yc_s, yc_r, yx_s, yx_r, yz_s, yz_r,
):
    h, e = lax.axis_index("ctx"), lax.axis_index("exp")
    z, c = e // 2, lax.rem(e, 2)
    half = res_ref.shape[1] // 2
    width = q_ref.shape[1]
    span = q_ref.shape[0]
    hid = gate.shape[1]
    chips = 4
    order = (2, 1, 3, 0)
    side = {"ctx": 1 - h, "exp": e}
    core = {"ctx": h, "exp": 2 * z + 1 - c}

    def at_z(dz):
        return lax.rem(z + dz, chips)

    def from_z(dz):
        return lax.rem(z + chips - dz, chips)

    def to(dz, other):
        return {"ctx": h, "exp": 2 * at_z(dz) + (1 - c if other else c)}

    started = []

    def link(src, dst, s, r, dev):
        return pltpu.make_async_remote_copy(
            src_ref=src, dst_ref=dst, send_sem=s, recv_sem=r, device_id=dev,
            device_id_type=pl.DeviceIdType.MESH,
        )

    def send(*args):
        copy = link(*args)
        copy.start()
        started.append(copy)
        return copy

    load_wo = pltpu.make_async_copy(wo_hbm, wy, w_sem.at[0])
    load_wo.start()
    loads = [
        pltpu.make_async_copy(gate_hbm.at[0], gate, w_sem.at[1]),
        pltpu.make_async_copy(up_hbm.at[0], up, w_sem.at[2]),
        pltpu.make_async_copy(down_hbm.at[0], down, w_sem.at[3]),
    ]

    barrier = pltpu.get_barrier_semaphore()
    pl.semaphore_signal(barrier, inc=1, device_id=side, device_id_type=pl.DeviceIdType.MESH)
    for dz in range(chips):
        for other in (False, True):
            if dz or other:
                pl.semaphore_signal(
                    barrier, inc=1, device_id=to(dz, other), device_id_type=pl.DeviceIdType.MESH
                )
    pl.semaphore_wait(barrier, 2 * chips)

    count = width // HEAD
    def state_link(i):
        rows = pl.ds(i * HEAD, HEAD)
        return link(state.at[rows], state_in.at[rows], state_s.at[i], state_r.at[i], side)

    def heads_link(i, b):
        cols = pl.ds(i * HEAD, HEAD)
        part = heads.at[b, :, cols]
        return link(part, part, heads_s.at[i], heads_r.at[i], side)

    @pl.when(h == 0)
    def _():
        for i in range(count):
            cols = slice(i * HEAD, (i + 1) * HEAD)
            own = lax.dot_general(
                k_ref[:, cols], v_ref[:, cols], (((0,), (0,)), ((), ())),
                preferred_element_type=F32,
            )
            state[cols, :] = own.astype(BF)
            state_link(i).start()

    keep = lax.broadcasted_iota(jnp.int32, (span, span), 0) >= lax.broadcasted_iota(
        jnp.int32, (span, span), 1
    )
    for i in range(count):
        cols = slice(i * HEAD, (i + 1) * HEAD)
        scores = lax.dot_general(
            q_ref[:, cols], k_ref[:, cols], (((1,), (1,)), ((), ())), preferred_element_type=F32
        )
        masked = jnp.where(keep, scores, 0.0).astype(BF)
        within[:, cols] = jnp.dot(masked, v_ref[:, cols], preferred_element_type=F32)
    for i in range(count):
        cols = slice(i * HEAD, (i + 1) * HEAD)

        @pl.when(h == 1)
        def _():
            state_link(i).wait_recv()
            within[:, cols] += jnp.dot(
                q_ref[:, cols], state_in[cols, :], preferred_element_type=F32
            )

        attended = within[:, cols]
        normed = attended * lax.rsqrt(
            jnp.mean(attended * attended, axis=-1, keepdims=True) + EPSILON
        )
        heads[h, :, cols] = normed.astype(BF)
        heads_link(i, h).start()
    peer_cols = pl.ds(pl.multiple_of((1 - h) * half, half), half)
    my_cols = pl.ds(pl.multiple_of(h * half, half), half)
    res_copy = send(res_ref.at[:, peer_cols], res_in, att_s.at[0], att_r.at[0], side)
    for load in loads:
        load.start()
    load_wo.wait()

    tile = 256

    def project(b):
        @pl.loop(0, half // tile)
        def _(n):
            cols = pl.ds(pl.multiple_of(n * tile, tile), tile)
            part = jnp.dot(heads[b], wy[:, cols], preferred_element_type=F32).astype(BF)
            term[b, :, :, cols] = part.reshape(span // ROWS, ROWS, tile)

    def core_term(dz, b):
        src = term.at[b, 2 * at_z(dz) + 1 - c]
        return (src, pair_in.at[dz, b], pair_s.at[dz, b], pair_r.at[dz, b], core)

    def ring_term(dz, b):
        k = dz - 1
        return (
            pair.at[k, b], ring_in.at[k, b], ring_s.at[k, b], ring_r.at[k, b], to(dz, False)
        )

    def scatter(b):
        for dz in order:
            send(*core_term(dz, b))
        for dz in order:
            link(*core_term(dz, b)).wait_recv()
            if dz:
                both = term[b, 2 * at_z(dz) + c].astype(F32) + pair_in[dz, b].astype(F32)
                pair[dz - 1, b] = both.astype(BF)
                send(*ring_term(dz, b))

    project(h)
    scatter(h)
    for i in range(count):
        heads_link(i, 1 - h).wait_recv()
    project(1 - h)
    scatter(1 - h)
    res_copy.wait_recv()
    def mixed(b):
        total = term[b, e].astype(F32) + pair_in[0, b].astype(F32)
        for dz in (1, 2, 3):
            link(*ring_term(dz, b)).wait_recv()
            total = total + ring_in[dz - 1, b].astype(F32)
        return total

    every[h, h, e] = (res_ref[:, my_cols].astype(F32) + mixed(h)).astype(BF)
    every[h, 1 - h, e] = (res_in[...].astype(F32) + mixed(1 - h)).astype(BF)

    def piece(side_half, owner):
        return every.at[side_half, :, owner]

    steps = []
    for k in range(1, chips):
        steps.append((z >= k, z - k, k - 1, 1))
        steps.append((z + k < chips, z + k, chips + k - 2, -1))

    def along(side_way, owner, slot):
        got = piece(h, 2 * owner + c)
        dev = {"ctx": h, "exp": 2 * (z + side_way) + c}
        return link(got, got, gz_s.at[slot], gz_r.at[slot], dev)

    def goes_on(side_way):
        return (z + side_way >= 0) & (z + side_way < chips)

    def to_side(owner):
        got = piece(h, 2 * owner + c)
        return link(got, got, gx_s.at[owner], gx_r.at[owner], side)

    def from_side(owner):
        got = piece(1 - h, 2 * owner + c)
        return link(got, got, gx_s.at[owner], gx_r.at[owner], side)

    def to_core(side_half, first, owner):
        got = piece(side_half, 2 * owner + c)
        return link(got, got, gc_s.at[first + owner], gc_r.at[first + owner], core)

    for side_way, slot in ((1, 0), (-1, chips - 1)):
        @pl.when(goes_on(side_way))
        def _():
            along(side_way, z, slot).start()

    to_side(z).start()
    to_core(h, 0, z).start()

    for there, owner, slot, side_way in steps:
        @pl.when(there)
        def _():
            along(side_way, owner, slot).wait_recv()

            if slot % (chips - 1) < chips - 2:
                @pl.when(goes_on(side_way))
                def _():
                    along(side_way, owner, slot + 1).start()

            to_side(owner).start()
            to_core(h, 0, owner).start()

    def pass_on(owner):
        from_side(owner).wait_recv()
        to_core(1 - h, chips, owner).start()

    def pass_step(there, owner):
        @pl.when(there)
        def _():
            pass_on(owner)

    def from_core(side_half, first, owner):
        got = piece(side_half, 2 * owner + 1 - c)
        link(got, got, gc_s.at[first + owner], gc_r.at[first + owner], core).wait_recv()

    def tiles(body):
        whole = hid // tile

        @pl.loop(0, whole)
        def _(n):
            body(pl.ds(pl.multiple_of(n * tile, tile), tile))

        if hid % tile:
            body(pl.ds(whole * tile, hid % tile))

    def product(side_half, weight, cols):
        rows = pl.ds(pl.multiple_of(side_half * half, half), half)
        return jnp.dot(
            every[side_half].reshape(2 * span, half), weight[rows, cols],
            preferred_element_type=F32,
        )

    pass_on(z)
    for there, owner, _, _ in steps[:2]:
        pass_step(there, owner)
    for owner in range(chips):
        from_core(h, 0, owner)
    loads[0].wait()

    def first_gate(cols):
        gate_sum[:, cols] = product(h, gate, cols)

    def first_up(cols):
        up_sum[:, cols] = product(h, up, cols)

    tiles(first_gate)
    for there, owner, _, _ in steps[2:4]:
        pass_step(there, owner)
    loads[1].wait()
    tiles(first_up)
    for there, owner, _, _ in steps[4:]:
        pass_step(there, owner)
    for owner in range(chips):
        from_core(1 - h, chips, owner)

    def second(cols):
        g = gate_sum[:, cols] + product(1 - h, gate, cols)
        u = up_sum[:, cols] + product(1 - h, up, cols)
        hidden[:, cols] = (g / (1.0 + jnp.exp(-g)) * u).astype(BF)

    tiles(second)
    loads[2].wait()

    def lower(side_half):
        @pl.loop(0, half // tile)
        def _(n):
            cols = pl.ds(pl.multiple_of(side_half * half + n * tile, tile), tile)
            part = jnp.dot(hidden[...], down[:, cols], preferred_element_type=F32)
            rows = pl.ds(pl.multiple_of(side_half * 2 * span, 2 * span), 2 * span)
            wy[rows, pl.ds(pl.multiple_of(n * tile, tile), tile)] = part.astype(BF)

    def rows_of(side_half, b, dz):
        first = side_half * 2 * span + b * span + 2 * ROWS * at_z(dz)
        return pl.ds(pl.multiple_of(first, 2 * ROWS), 2 * ROWS)

    def core_link(dz, b):
        return (
            wy.at[rows_of(1 - c, b, dz)], core_in.at[dz, b], yc_s.at[dz, b], yc_r.at[dz, b], core
        )

    lower(1 - c)
    for b in (1 - h, h):
        for dz in order:
            send(*core_link(dz, b))
    lower(c)
    for dz in order:
        link(*core_link(dz, 1 - h)).wait_recv()
        side_out[dz] = (
            wy[rows_of(c, 1 - h, dz)].astype(F32) + core_in[dz, 1 - h].astype(F32)
        ).astype(BF)
        send(side_out.at[dz], side_in.at[dz], yx_s.at[dz], yx_r.at[dz], side)

    def out_link(dz, other):
        if dz:
            part = 1 - c if other else c
            src = ready.at[dz, pl.ds(pl.multiple_of(part * ROWS, ROWS), ROWS)]
        else:
            src = ready.at[dz, pl.ds(pl.multiple_of((1 - c) * ROWS, ROWS), ROWS)]
        o = int(other)
        return (src, back.at[dz, o], yz_s.at[dz, o], yz_r.at[dz, o], to(dz, other))

    for dz in order:
        link(side_out.at[dz], side_in.at[dz], yx_s.at[dz], yx_r.at[dz], side).wait_recv()
        link(*core_link(dz, h)).wait_recv()
        ready[dz] = (
            wy[rows_of(c, h, dz)].astype(F32)
            + core_in[dz, h].astype(F32)
            + side_in[dz].astype(F32)
        ).astype(BF)
        for other in (False, True):
            if dz or other:
                send(*out_link(dz, other))

    logits = jnp.zeros((router_ref.shape[0], ROWS), F32)
    for s in range(2):
        logits = logits + lax.dot_general(
            router_ref[:, s * half:(s + 1) * half], every[s, h, e],
            (((1,), (1,)), ((), ())), preferred_element_type=F32,
        )
    lines = lax.broadcasted_iota(jnp.int32, logits.shape, 0)
    one = (ids_ref[0:1, :] == lines).astype(F32)
    two = (ids_ref[1:2, :] == lines).astype(F32)
    gap = jnp.sum((one - two) * logits, axis=0, keepdims=True)
    leading = 1.0 / (1.0 + jnp.exp(-gap))
    share = leading * one + (1.0 - leading) * two
    diagonal = lax.broadcasted_iota(jnp.int32, (ROWS, ROWS), 0) == lax.broadcasted_iota(
        jnp.int32, (ROWS, ROWS), 1
    )

    def weight_of(dz):
        row = jnp.sum(jnp.where(lines == from_z(dz), share, 0.0), axis=0, keepdims=True)
        return jnp.sum(jnp.where(diagonal, row, 0.0), axis=1, keepdims=True)

    weights = [weight_of(dz) for dz in range(chips)]
    for other in (False, True):
        for dz in order:
            if dz or other:
                link(*out_link(dz, other)).wait_recv()
        part = 1 - c if other else c
        total = every[part, h, e].astype(F32)
        for dz in range(chips):
            if dz or other:
                value = back[dz, int(other)]
            else:
                value = ready[0, pl.ds(pl.multiple_of(c * ROWS, ROWS), ROWS)]
            total = total + weights[dz] * value.astype(F32)
        out_ref[:, pl.ds(pl.multiple_of(part * half, half), half)] = total.astype(BF)
    for copy in started:
        copy.wait_send()

    @pl.when(h == 0)
    def _():
        for i in range(count):
            state_link(i).wait_send()

    for i in range(count):
        heads_link(i, h).wait_send()
    for side_way, slot in ((1, 0), (-1, chips - 1)):
        @pl.when(goes_on(side_way))
        def _():
            along(side_way, z, slot).wait_send()

    for there, owner, slot, side_way in steps:
        if slot % (chips - 1) < chips - 2:
            @pl.when(there & goes_on(side_way))
            def _():
                along(side_way, owner, slot + 1).wait_send()

    for owner in range(chips):
        to_side(owner).wait_send()
        to_core(h, 0, owner).wait_send()
        to_core(1 - h, chips, owner).wait_send()


def per_device_fused(
    queries, key_vecs, values, residual, out_weight, router_weight, expert_ids,
    gate_weight, up_weight, down_weight,
):
    span, width = queries.shape
    half = out_weight.shape[1]
    model = residual.shape[1]
    hid = gate_weight.shape[2]
    blocks = span // ROWS
    count = width // HEAD
    vmem, sem = pltpu.VMEM, pltpu.SemaphoreType.DMA
    in_vmem = pl.BlockSpec(memory_space=pltpu.VMEM)
    in_hbm = pl.BlockSpec(memory_space=pl.ANY)
    return pl.pallas_call(
        layer_kernel,
        out_shape=jax.ShapeDtypeStruct(residual.shape, BF),
        in_specs=[in_vmem] * 4 + [in_hbm] + [in_vmem] * 2 + [in_hbm] * 3,
        out_specs=in_vmem,
        scratch_shapes=[
            vmem((width, half), BF),
            vmem((model, hid), BF),
            vmem((model, hid), BF),
            vmem((hid, model), BF),
            vmem((width, HEAD), BF),
            vmem((width, HEAD), BF),
            vmem((span, width), F32),
            vmem((2, span, width), BF),
            vmem((ROWS, half), BF),
            vmem((2, blocks, ROWS, half), BF),
            vmem((4, 2, ROWS, half), BF),
            vmem((3, 2, ROWS, half), BF),
            vmem((3, 2, ROWS, half), BF),
            vmem((2, 2, blocks, ROWS, half), BF),
            vmem((2 * span, hid), F32),
            vmem((2 * span, hid), F32),
            vmem((2 * span, hid), BF),
            vmem((4, 2, 2 * ROWS, half), BF),
            vmem((4, 2 * ROWS, half), BF),
            vmem((4, 2 * ROWS, half), BF),
            vmem((4, 2 * ROWS, half), BF),
            vmem((4, 2, ROWS, half), BF),
            sem((4,)), sem((count,)), sem((count,)), sem((count,)), sem((count,)), sem((1,)), sem((1,)),
            sem((4, 2)), sem((4, 2)), sem((3, 2)), sem((3, 2)),
            sem((6,)), sem((6,)), sem((4,)), sem((4,)), sem((8,)), sem((8,)),
            sem((4, 2)), sem((4, 2)), sem((4,)), sem((4,)), sem((4, 2)), sem((4, 2)),
        ],
        compiler_params=pltpu.CompilerParams(
            collective_id=0, has_side_effects=True, vmem_limit_bytes=VMEM_BYTES
        ),
    )(
        queries, key_vecs, values, residual, out_weight, router_weight.T, expert_ids.T,
        gate_weight, up_weight, down_weight,
    )


VMEM_BYTES = 66 * 1000 * 1000


def solution(mesh):
    fused = mesh.shape["ctx"] == 2 and mesh.shape["exp"] == 8
    body = per_device_fused if fused else per_device
    in_specs = (
        P(("dp", "ctx"), "exp"),
        P(("dp", "ctx"), "exp"),
        P(("dp", "ctx"), "exp"),
        P(("dp", "ctx", "exp"), None),
        P("exp", "ctx"),
        P(),
        P(("dp", "ctx", "exp"), None),
        P("exp", None, "ctx"),
        P("exp", None, "ctx"),
        P("exp", "ctx", None),
    )
    out_specs = P(("dp", "ctx", "exp"), None)
    return jax.shard_map(
        body, mesh=mesh, in_specs=in_specs, out_specs=out_specs, check_vma=False
    )
```

```python
import jax
import jax.numpy as jnp
from jax import lax
from jax.experimental import pallas as pl
from jax.experimental.pallas import tpu as pltpu
from jax.sharding import PartitionSpec as P

HEAD = 128


EPSILON = 1e-06


def carried_in(value, axis, combine, identity):
    peers, position = (lax.axis_size(axis), lax.axis_index(axis))
    everything = lax.all_gather(value.astype(jnp.bfloat16), axis)
    start = jnp.broadcast_to(jnp.asarray(identity, value.dtype), value.shape)

    def lap(k, before):
        reached = k < position
        new = combine(before, everything[k].astype(value.dtype))
        return jnp.where(reached, new, before)

    return lax.fori_loop(0, peers, lap, start)


def expert_rows(tokens, gate_half, up_half, down_half):
    gate_part = jnp.dot(tokens, gate_half, preferred_element_type=jnp.float32)
    up_part = jnp.dot(tokens, up_half, preferred_element_type=jnp.float32)
    hidden = (jax.nn.silu(gate_part) * up_part).astype(jnp.bfloat16)
    return jnp.dot(hidden, down_half, preferred_element_type=jnp.float32)


def add_states(first, second):
    return first + second


def per_device(
    queries,
    key_vecs,
    values,
    residual,
    out_weight,
    router_weight,
    expert_ids,
    gate_weight,
    up_weight,
    down_weight,
):
    ctx_count = lax.axis_size("ctx")
    exp_count = lax.axis_size("exp")
    span_len, local_width = queries.shape
    head_local = local_width // HEAD
    q_heads = queries.reshape(span_len, head_local, HEAD)
    k_heads = key_vecs.reshape(span_len, head_local, HEAD)
    v_heads = values.reshape(span_len, head_local, HEAD)
    scores = jnp.einsum("thd,shd->hts", q_heads, k_heads, preferred_element_type=jnp.float32)
    causal = jnp.arange(span_len)[:, None] >= jnp.arange(span_len)[None, :]
    masked = jnp.where(causal[None], scores, jnp.float32(0.0)).astype(jnp.bfloat16)
    within = jnp.einsum("hts,shd->thd", masked, v_heads, preferred_element_type=jnp.float32)
    own_state = jnp.einsum("shd,she->hde", k_heads, v_heads, preferred_element_type=jnp.float32)
    earlier = carried_in(own_state, "ctx", add_states, jnp.zeros_like(own_state))
    carried = jnp.einsum(
        "thd,hde->the", q_heads, earlier.astype(jnp.bfloat16), preferred_element_type=jnp.float32
    )
    attended = within + carried
    normed = attended * lax.rsqrt(jnp.mean(attended * attended, axis=-1, keepdims=True) + EPSILON)
    heads_out = normed.astype(jnp.bfloat16).reshape(span_len, local_width)
    projected = jnp.dot(
        heads_out,
        lax.all_gather(out_weight, "ctx", axis=1, tiled=True),
        preferred_element_type=jnp.float32,
    )
    mixed = lax.psum_scatter(
        projected.astype(jnp.bfloat16), "exp", scatter_dimension=0, tiled=True
    ).astype(jnp.float32)
    hidden_in = (residual.astype(jnp.float32) + mixed).astype(jnp.bfloat16)
    token_count, model_width = hidden_in.shape
    expert_count = router_weight.shape[1]
    capacity = min(token_count, 3 * token_count // expert_count)
    logits = jnp.dot(hidden_in, router_weight, preferred_element_type=jnp.float32)
    chosen = (expert_ids[:, :, None] == jnp.arange(expert_count)[None, None, :]).astype(jnp.float32)
    picked = jnp.sum(chosen * logits[:, None, :], axis=-1)
    leading = jax.nn.sigmoid(picked[:, 0] - picked[:, 1])
    mixing = jnp.stack([leading, 1.0 - leading], axis=1)
    entries = chosen.reshape(2 * token_count, expert_count)
    position = jnp.arange(2 * token_count)
    earlier_mask = (position[:, None] > position[None, :]).astype(jnp.float32)
    ranks = jnp.dot(earlier_mask, entries, precision=lax.Precision.HIGHEST)
    slot_of = jnp.sum(ranks * entries, axis=-1).reshape(token_count, 2)
    slot_hot = (
        slot_of[:, :, None] == jnp.arange(capacity).astype(jnp.float32)[None, None, :]
    ).astype(jnp.float32)
    placed = chosen[:, :, :, None] * slot_hot[:, :, None, :]
    dispatch = jnp.sum(placed, axis=1).astype(jnp.bfloat16)
    combine = jnp.sum(placed * mixing[:, :, None, None], axis=1)
    packed = jnp.einsum(
        "tes,td->esd", dispatch, hidden_in, preferred_element_type=jnp.float32
    ).astype(jnp.bfloat16)
    outgoing = jnp.repeat(packed, 2, axis=0)
    gate_half = gate_weight[0]
    up_half = up_weight[0]
    down_half = down_weight[0]
    fanned = jnp.broadcast_to(outgoing[None], (ctx_count,) + outgoing.shape).reshape(
        ctx_count * exp_count, capacity, model_width
    )
    arrived = lax.all_to_all(fanned, ("ctx", "exp"), split_axis=0, concat_axis=0, tiled=True)
    flattened = arrived.reshape(-1, model_width)
    partial_value = expert_rows(flattened, gate_half, up_half, down_half).reshape(arrived.shape)
    reduced = lax.psum_scatter(
        partial_value.reshape(ctx_count * exp_count * capacity, model_width).astype(jnp.bfloat16),
        "ctx",
        scatter_dimension=0,
        tiled=True,
    ).astype(jnp.float32)
    returned = lax.all_to_all(
        reduced.reshape(exp_count, capacity, model_width).astype(jnp.bfloat16),
        "exp",
        split_axis=0,
        concat_axis=0,
        tiled=True,
    ).astype(jnp.float32)
    summed = jnp.sum(returned.reshape(expert_count, 2, capacity, model_width), axis=1)
    expert_out = jnp.einsum(
        "tes,esd->td",
        combine,
        summed,
        precision=lax.Precision.HIGHEST,
        preferred_element_type=jnp.float32,
    )
    return (hidden_in.astype(jnp.float32) + expert_out).astype(jnp.bfloat16)


BF, F32 = jnp.bfloat16, jnp.float32
ROWS = 16


def layer_kernel(
    q_ref, k_ref, v_ref, res_ref, wo_hbm, router_ref, ids_ref, gate_hbm, up_hbm, down_hbm,
    out_ref,
    wy, gate, up, down, state, state_in, within, heads, res_in, term, pair_in, pair, ring_in,
    every, gate_sum, up_sum, hidden, core_in, side_out, side_in, ready, back,
    w_sem, state_s, state_r, heads_s, heads_r, att_s, att_r, pair_s, pair_r, ring_s, ring_r,
    gz_s, gz_r, gx_s, gx_r, gc_s, gc_r, yc_s, yc_r, yx_s, yx_r, yz_s, yz_r,
):
    h, e = lax.axis_index("ctx"), lax.axis_index("exp")
    z, c = e // 2, lax.rem(e, 2)
    half = res_ref.shape[1] // 2
    width = q_ref.shape[1]
    span = q_ref.shape[0]
    hid = gate.shape[1]
    chips = 4
    order = (2, 1, 3, 0)
    side = {"ctx": 1 - h, "exp": e}
    core = {"ctx": h, "exp": 2 * z + 1 - c}

    def at_z(dz):
        return lax.rem(z + dz, chips)

    def from_z(dz):
        return lax.rem(z + chips - dz, chips)

    def to(dz, other):
        return {"ctx": h, "exp": 2 * at_z(dz) + (1 - c if other else c)}

    started = []

    def link(src, dst, s, r, dev):
        return pltpu.make_async_remote_copy(
            src_ref=src, dst_ref=dst, send_sem=s, recv_sem=r, device_id=dev,
            device_id_type=pl.DeviceIdType.MESH,
        )

    def send(*args):
        copy = link(*args)
        copy.start()
        started.append(copy)
        return copy

    load_wo = pltpu.make_async_copy(wo_hbm, wy, w_sem.at[0])
    load_wo.start()
    loads = [
        pltpu.make_async_copy(gate_hbm.at[0], gate, w_sem.at[1]),
        pltpu.make_async_copy(up_hbm.at[0], up, w_sem.at[2]),
        pltpu.make_async_copy(down_hbm.at[0], down, w_sem.at[3]),
    ]

    barrier = pltpu.get_barrier_semaphore()
    pl.semaphore_signal(barrier, inc=1, device_id=side, device_id_type=pl.DeviceIdType.MESH)
    for dz in range(chips):
        for other in (False, True):
            if dz or other:
                pl.semaphore_signal(
                    barrier, inc=1, device_id=to(dz, other), device_id_type=pl.DeviceIdType.MESH
                )
    pl.semaphore_wait(barrier, 2 * chips)

    count = width // HEAD
    def state_link(i):
        rows = pl.ds(i * HEAD, HEAD)
        return link(state.at[rows], state_in.at[rows], state_s.at[i], state_r.at[i], side)

    def heads_link(i, b):
        cols = pl.ds(i * HEAD, HEAD)
        part = heads.at[b, :, cols]
        return link(part, part, heads_s.at[i], heads_r.at[i], side)

    @pl.when(h == 0)
    def _():
        for i in range(count):
            cols = slice(i * HEAD, (i + 1) * HEAD)
            own = lax.dot_general(
                k_ref[:, cols], v_ref[:, cols], (((0,), (0,)), ((), ())),
                preferred_element_type=F32,
            )
            state[cols, :] = own.astype(BF)
            state_link(i).start()

    keep = lax.broadcasted_iota(jnp.int32, (span, span), 0) >= lax.broadcasted_iota(
        jnp.int32, (span, span), 1
    )
    for i in range(count):
        cols = slice(i * HEAD, (i + 1) * HEAD)
        scores = lax.dot_general(
            q_ref[:, cols], k_ref[:, cols], (((1,), (1,)), ((), ())), preferred_element_type=F32
        )
        masked = jnp.where(keep, scores, 0.0).astype(BF)
        within[:, cols] = jnp.dot(masked, v_ref[:, cols], preferred_element_type=F32)
    for i in range(count):
        cols = slice(i * HEAD, (i + 1) * HEAD)

        @pl.when(h == 1)
        def _():
            state_link(i).wait_recv()
            within[:, cols] += jnp.dot(
                q_ref[:, cols], state_in[cols, :], preferred_element_type=F32
            )

        attended = within[:, cols]
        normed = attended * lax.rsqrt(
            jnp.mean(attended * attended, axis=-1, keepdims=True) + EPSILON
        )
        heads[h, :, cols] = normed.astype(BF)
        heads_link(i, h).start()
    peer_cols = pl.ds(pl.multiple_of((1 - h) * half, half), half)
    my_cols = pl.ds(pl.multiple_of(h * half, half), half)
    res_copy = send(res_ref.at[:, peer_cols], res_in, att_s.at[0], att_r.at[0], side)
    for load in loads:
        load.start()
    load_wo.wait()

    tile = 256

    def project(b):
        @pl.loop(0, half // tile)
        def _(n):
            cols = pl.ds(pl.multiple_of(n * tile, tile), tile)
            part = jnp.dot(heads[b], wy[:, cols], preferred_element_type=F32).astype(BF)
            term[b, :, :, cols] = part.reshape(span // ROWS, ROWS, tile)

    def core_term(dz, b):
        src = term.at[b, 2 * at_z(dz) + 1 - c]
        return (src, pair_in.at[dz, b], pair_s.at[dz, b], pair_r.at[dz, b], core)

    def ring_term(dz, b):
        k = dz - 1
        return (
            pair.at[k, b], ring_in.at[k, b], ring_s.at[k, b], ring_r.at[k, b], to(dz, False)
        )

    def scatter(b):
        for dz in order:
            send(*core_term(dz, b))
        for dz in order:
            link(*core_term(dz, b)).wait_recv()
            if dz:
                both = term[b, 2 * at_z(dz) + c].astype(F32) + pair_in[dz, b].astype(F32)
                pair[dz - 1, b] = both.astype(BF)
                send(*ring_term(dz, b))

    project(h)
    scatter(h)
    for i in range(count):
        heads_link(i, 1 - h).wait_recv()
    project(1 - h)
    scatter(1 - h)
    def mixed(b):
        total = term[b, e].astype(F32) + pair_in[0, b].astype(F32)
        for dz in (1, 2, 3):
            link(*ring_term(dz, b)).wait_recv()
            total = total + ring_in[dz - 1, b].astype(F32)
        return total

    steps = []
    for k in range(1, chips):
        steps.append((z >= k, z - k, k - 1, 1))
        steps.append((z + k < chips, z + k, chips + k - 2, -1))

    def along(side_way, owner, slot, b):
        got = every.at[h, b, 2 * owner + c]
        dev = {"ctx": h, "exp": 2 * (z + side_way) + c}
        return link(got, got, gz_s.at[slot, b], gz_r.at[slot, b], dev)

    def goes_on(side_way):
        return (z + side_way >= 0) & (z + side_way < chips)

    def to_side(owner, b):
        got = every.at[h, b, 2 * owner + c]
        return link(got, got, gx_s.at[owner, b], gx_r.at[owner, b], side)

    def from_side(owner, b):
        got = every.at[1 - h, b, 2 * owner + c]
        return link(got, got, gx_s.at[owner, b], gx_r.at[owner, b], side)

    def to_core(side_half, first, owner, b):
        got = every.at[side_half, b, 2 * owner + c]
        return link(got, got, gc_s.at[first + owner, b], gc_r.at[first + owner, b], core)

    def spread(b):
        for side_way, slot in ((1, 0), (-1, chips - 1)):
            @pl.when(goes_on(side_way))
            def _():
                along(side_way, z, slot, b).start()

        to_side(z, b).start()
        to_core(h, 0, z, b).start()

    def forward(some, b):
        for there, owner, slot, side_way in some:
            @pl.when(there)
            def _():
                along(side_way, owner, slot, b).wait_recv()

                if slot % (chips - 1) < chips - 2:
                    @pl.when(goes_on(side_way))
                    def _():
                        along(side_way, owner, slot + 1, b).start()

                to_side(owner, b).start()
                to_core(h, 0, owner, b).start()

    def pass_on(owner, b):
        from_side(owner, b).wait_recv()
        to_core(1 - h, chips, owner, b).start()

    def pass_steps(some, b):
        for there, owner, _, _ in some:
            @pl.when(there)
            def _():
                pass_on(owner, b)

    def from_core(side_half, first, owner, b):
        got = every.at[side_half, b, 2 * owner + 1 - c]
        link(got, got, gc_s.at[first + owner, b], gc_r.at[first + owner, b], core).wait_recv()

    every[h, h, e] = (res_ref[:, my_cols].astype(F32) + mixed(h)).astype(BF)
    spread(h)
    forward(steps[:2], h)
    res_copy.wait_recv()
    every[h, 1 - h, e] = (res_in[...].astype(F32) + mixed(1 - h)).astype(BF)
    spread(1 - h)
    forward(steps[2:], h)
    forward(steps, 1 - h)

    def tiles(body):
        whole = hid // tile

        @pl.loop(0, whole)
        def _(n):
            body(pl.ds(pl.multiple_of(n * tile, tile), tile))

        if hid % tile:
            body(pl.ds(whole * tile, hid % tile))

    def product(side_half, weight, cols):
        rows = pl.ds(pl.multiple_of(side_half * half, half), half)
        return jnp.dot(
            every[side_half].reshape(2 * span, half), weight[rows, cols],
            preferred_element_type=F32,
        )

    pass_on(z, 1 - h)
    pass_steps(steps, 1 - h)
    pass_on(z, h)
    for b in range(2):
        for owner in range(chips):
            from_core(h, 0, owner, b)
    loads[0].wait()

    def first_gate(cols):
        gate_sum[:, cols] = product(h, gate, cols)

    def first_up(cols):
        up_sum[:, cols] = product(h, up, cols)

    tiles(first_gate)
    pass_steps(steps[:4], h)
    loads[1].wait()
    tiles(first_up)
    pass_steps(steps[4:], h)
    for b in range(2):
        for owner in range(chips):
            from_core(1 - h, chips, owner, b)

    def second(cols):
        g = gate_sum[:, cols] + product(1 - h, gate, cols)
        u = up_sum[:, cols] + product(1 - h, up, cols)
        hidden[:, cols] = (g / (1.0 + jnp.exp(-g)) * u).astype(BF)

    tiles(second)
    loads[2].wait()

    def lower(side_half):
        @pl.loop(0, half // tile)
        def _(n):
            cols = pl.ds(pl.multiple_of(side_half * half + n * tile, tile), tile)
            part = jnp.dot(hidden[...], down[:, cols], preferred_element_type=F32)
            rows = pl.ds(pl.multiple_of(side_half * 2 * span, 2 * span), 2 * span)
            wy[rows, pl.ds(pl.multiple_of(n * tile, tile), tile)] = part.astype(BF)

    def rows_of(side_half, b, dz):
        first = side_half * 2 * span + b * span + 2 * ROWS * at_z(dz)
        return pl.ds(pl.multiple_of(first, 2 * ROWS), 2 * ROWS)

    def core_link(dz, b):
        return (
            wy.at[rows_of(1 - c, b, dz)], core_in.at[dz, b], yc_s.at[dz, b], yc_r.at[dz, b], core
        )

    def part_rows(other):
        part = 1 - c if other else c
        return pl.ds(pl.multiple_of(part * ROWS, ROWS), ROWS)

    def side_link(dz, other):
        rows, o = part_rows(other), int(other)
        return (
            side_out.at[dz, rows], side_in.at[dz, rows], yx_s.at[dz, o], yx_r.at[dz, o], side
        )

    def owner_rows(side_half, b, dz, other):
        part = 1 - c if other else c
        first = side_half * 2 * span + b * span + ROWS * (2 * at_z(dz) + part)
        return pl.ds(pl.multiple_of(first, ROWS), ROWS)

    lower(1 - c)
    for b in (1 - h, h):
        for dz in order:
            send(*core_link(dz, b))
    lower(c)
    for dz in order:
        link(*core_link(dz, 1 - h)).wait_recv()
        side_out[dz] = (
            wy[rows_of(c, 1 - h, dz)].astype(F32) + core_in[dz, 1 - h].astype(F32)
        ).astype(BF)
        for other in (False, True):
            send(*side_link(dz, other))

    def out_link(dz, other):
        o = int(other)
        return (
            ready.at[dz, part_rows(other)], back.at[dz, o], yz_s.at[dz, o], yz_r.at[dz, o],
            to(dz, other),
        )

    for dz in order:
        link(*core_link(dz, h)).wait_recv()
        for other in (False, True):
            rows = part_rows(other)
            link(*side_link(dz, other)).wait_recv()
            ready[dz, rows] = (
                wy[owner_rows(c, h, dz, other)].astype(F32)
                + core_in[dz, h, rows].astype(F32)
                + side_in[dz, rows].astype(F32)
            ).astype(BF)
            if dz or other:
                send(*out_link(dz, other))

    logits = jnp.zeros((router_ref.shape[0], ROWS), F32)
    for s in range(2):
        logits = logits + lax.dot_general(
            router_ref[:, s * half:(s + 1) * half], every[s, h, e],
            (((1,), (1,)), ((), ())), preferred_element_type=F32,
        )
    lines = lax.broadcasted_iota(jnp.int32, logits.shape, 0)
    one = (ids_ref[0:1, :] == lines).astype(F32)
    two = (ids_ref[1:2, :] == lines).astype(F32)
    gap = jnp.sum((one - two) * logits, axis=0, keepdims=True)
    leading = 1.0 / (1.0 + jnp.exp(-gap))
    share = leading * one + (1.0 - leading) * two
    diagonal = lax.broadcasted_iota(jnp.int32, (ROWS, ROWS), 0) == lax.broadcasted_iota(
        jnp.int32, (ROWS, ROWS), 1
    )

    def weight_of(dz):
        row = jnp.sum(jnp.where(lines == from_z(dz), share, 0.0), axis=0, keepdims=True)
        return jnp.sum(jnp.where(diagonal, row, 0.0), axis=1, keepdims=True)

    weights = [weight_of(dz) for dz in range(chips)]
    for other in (False, True):
        for dz in order:
            if dz or other:
                link(*out_link(dz, other)).wait_recv()
        part = 1 - c if other else c
        total = every[part, h, e].astype(F32)
        for dz in range(chips):
            if dz or other:
                value = back[dz, int(other)]
            else:
                value = ready[0, pl.ds(pl.multiple_of(c * ROWS, ROWS), ROWS)]
            total = total + weights[dz] * value.astype(F32)
        out_ref[:, pl.ds(pl.multiple_of(part * half, half), half)] = total.astype(BF)
    for copy in started:
        copy.wait_send()

    @pl.when(h == 0)
    def _():
        for i in range(count):
            state_link(i).wait_send()

    for i in range(count):
        heads_link(i, h).wait_send()
    for b in range(2):
        for side_way, slot in ((1, 0), (-1, chips - 1)):
            @pl.when(goes_on(side_way))
            def _():
                along(side_way, z, slot, b).wait_send()

        for there, owner, slot, side_way in steps:
            if slot % (chips - 1) < chips - 2:
                @pl.when(there & goes_on(side_way))
                def _():
                    along(side_way, owner, slot + 1, b).wait_send()

        for owner in range(chips):
            to_side(owner, b).wait_send()
            to_core(h, 0, owner, b).wait_send()
            to_core(1 - h, chips, owner, b).wait_send()


def per_device_fused(
    queries, key_vecs, values, residual, out_weight, router_weight, expert_ids,
    gate_weight, up_weight, down_weight,
):
    span, width = queries.shape
    half = out_weight.shape[1]
    model = residual.shape[1]
    hid = gate_weight.shape[2]
    blocks = span // ROWS
    count = width // HEAD
    vmem, sem = pltpu.VMEM, pltpu.SemaphoreType.DMA
    in_vmem = pl.BlockSpec(memory_space=pltpu.VMEM)
    in_hbm = pl.BlockSpec(memory_space=pl.ANY)
    return pl.pallas_call(
        layer_kernel,
        out_shape=jax.ShapeDtypeStruct(residual.shape, BF),
        in_specs=[in_vmem] * 4 + [in_hbm] + [in_vmem] * 2 + [in_hbm] * 3,
        out_specs=in_vmem,
        scratch_shapes=[
            vmem((width, half), BF),
            vmem((model, hid), BF),
            vmem((model, hid), BF),
            vmem((hid, model), BF),
            vmem((width, HEAD), BF),
            vmem((width, HEAD), BF),
            vmem((span, width), F32),
            vmem((2, span, width), BF),
            vmem((ROWS, half), BF),
            vmem((2, blocks, ROWS, half), BF),
            vmem((4, 2, ROWS, half), BF),
            vmem((3, 2, ROWS, half), BF),
            vmem((3, 2, ROWS, half), BF),
            vmem((2, 2, blocks, ROWS, half), BF),
            vmem((2 * span, hid), F32),
            vmem((2 * span, hid), F32),
            vmem((2 * span, hid), BF),
            vmem((4, 2, 2 * ROWS, half), BF),
            vmem((4, 2 * ROWS, half), BF),
            vmem((4, 2 * ROWS, half), BF),
            vmem((4, 2 * ROWS, half), BF),
            vmem((4, 2, ROWS, half), BF),
            sem((4,)), sem((count,)), sem((count,)), sem((count,)), sem((count,)), sem((1,)), sem((1,)),
            sem((4, 2)), sem((4, 2)), sem((3, 2)), sem((3, 2)),
            sem((6, 2)), sem((6, 2)), sem((4, 2)), sem((4, 2)), sem((8, 2)), sem((8, 2)),
            sem((4, 2)), sem((4, 2)), sem((4, 2)), sem((4, 2)), sem((4, 2)), sem((4, 2)),
        ],
        compiler_params=pltpu.CompilerParams(
            collective_id=0, has_side_effects=True, vmem_limit_bytes=VMEM_BYTES
        ),
    )(
        queries, key_vecs, values, residual, out_weight, router_weight.T, expert_ids.T,
        gate_weight, up_weight, down_weight,
    )


VMEM_BYTES = 66 * 1000 * 1000


def solution(mesh):
    fused = mesh.shape["ctx"] == 2 and mesh.shape["exp"] == 8
    body = per_device_fused if fused else per_device
    in_specs = (
        P(("dp", "ctx"), "exp"),
        P(("dp", "ctx"), "exp"),
        P(("dp", "ctx"), "exp"),
        P(("dp", "ctx", "exp"), None),
        P("exp", "ctx"),
        P(),
        P(("dp", "ctx", "exp"), None),
        P("exp", None, "ctx"),
        P("exp", None, "ctx"),
        P("exp", "ctx", None),
    )
    out_specs = P(("dp", "ctx", "exp"), None)
    return jax.shard_map(
        body, mesh=mesh, in_specs=in_specs, out_specs=out_specs, check_vma=False
    )
```
